128 devices in a mesh: pool: 4 (over y), seq: 32 (over x, z, core).
Axes of the slice: x: 4, y: 4, z: 4, core: 2. Of those that a mesh axis runs over, the one named last changes fastest.
Arguments:
- pool_kv: bfloat16 [16, 4096, 1024], P('pool', 'seq'), may hold values from -4 to 4
- span_home: int32 [12], replicated, may hold values from 0 to 15, as said below
- span_order: int32 [4, 3], P('pool'), may hold values from 0 to 11, as said below
- chosen: int32 [4, 14], P('pool'), may hold values from 0 to 95, as said below
- fresh_q: bfloat16 [4, 1792, 6144], P('pool', 'seq'), may hold values from -300 to 300
- fresh_kv: bfloat16 [4, 1792, 1024], P('pool', 'seq'), may hold values from -5 to 5
Outputs:
- attended: bfloat16 [4, 1792, 6144], P('pool', 'seq')
- decode_kv: bfloat16 [4, 32, 4, 96, 1024], P('pool', 'seq')
The draws below stay inside these ranges and needn't reach their ends.
Inputs may be any that keep to these rules, and one draw needn't show every extreme that they name: `span_home`: all entries differ; home // 4 is the replica of a passage, and the 3 passages r * 3 to r * 3 + 2 of request r lie on different replicas; some replica holds a passage of every request. `span_order`: row r orders the passages r * 3 to r * 3 + 2. `chosen`: each row lists 14 different blocks in rising order; block k holds positions k * 128 to k * 128 + 127.
All inputs are finite; a program needn't handle non-finite values.
Results may differ from the reference program's by a relative error of at most 0.0035.
Values may be sent and summed in bfloat16 or wider, within the bound.
A program may use at most 192 MiB of HBM per device.

```python
import jax
import jax.numpy as jnp
from jax import lax

HEADS = 48
KV_HEADS = 4
HEAD_DIM = 128
BLOCK = 128
SPANS = 3
GROUP = 12
REQUESTS = 4
SLOTS = 4
SPAN_LEN = 4096
BLOCKS = 96
SELECTED = 14
PICKED_ROWS = 1792
RUN = 4
N_POOL = 4
N_SEQ = 32


def draw_span_home(key, part):
    favored = jax.random.randint(jax.random.fold_in(key, 1), (), 0, REQUESTS)
    replicas = jnp.arange(REQUESTS, dtype=jnp.int32)
    raw_score = jax.random.randint(jax.random.fold_in(key, 2), (REQUESTS, REQUESTS), 0, 1024)
    scores = (raw_score + 2048 * (replicas[None, :] == favored).astype(jnp.int32)) * REQUESTS + replicas[None, :]
    ranked = jnp.argsort(-scores, axis=1)
    picked_rep = ranked[:, :SPANS].astype(jnp.int32)
    slot_score = jax.random.randint(jax.random.fold_in(key, 3), (REQUESTS, SLOTS), 0, 1 << 20) * SLOTS + jnp.arange(SLOTS, dtype=jnp.int32)[None, :]
    slot_perm = jnp.argsort(slot_score, axis=1).astype(jnp.int32)
    owners = jnp.broadcast_to(jnp.arange(REQUESTS, dtype=jnp.int32)[:, None], (REQUESTS, SPANS))
    slot_of = slot_perm[picked_rep, owners]
    return (picked_rep * SLOTS + slot_of).reshape(REQUESTS * SPANS).astype(jnp.int32)


def draw_span_order(key, part):
    scores = jax.random.randint(jax.random.fold_in(key, 21), (REQUESTS, SPANS), 0, 1 << 20) * SPANS + jnp.arange(SPANS, dtype=jnp.int32)[None, :]
    ranked = jnp.argsort(scores, axis=1).astype(jnp.int32)
    return (ranked + jnp.arange(REQUESTS, dtype=jnp.int32)[:, None] * SPANS).astype(jnp.int32)


def draw_chosen(key, part):
    scores = jax.random.randint(jax.random.fold_in(key, 31), (REQUESTS, BLOCKS), 0, 1 << 20) * BLOCKS + jnp.arange(BLOCKS, dtype=jnp.int32)[None, :]
    ranked = jnp.argsort(scores, axis=1)[:, :SELECTED]
    return jnp.sort(ranked, axis=1).astype(jnp.int32)


def fresh_pair(key):
    row_total = PICKED_ROWS
    base = jnp.clip(jax.random.normal(jax.random.fold_in(key, 101), (REQUESTS, row_total, KV_HEADS, 2, HEAD_DIM), jnp.float32), -4.0, 4.0)
    query = 3.0 * jnp.clip(jax.random.normal(jax.random.fold_in(key, 102), (REQUESTS, row_total, KV_HEADS, GROUP, HEAD_DIM), jnp.float32), -4.0, 4.0)
    query = jnp.clip(query, -300.0, 300.0).reshape(REQUESTS, row_total, HEADS * HEAD_DIM)
    base = jnp.clip(base, -5.0, 5.0).reshape(REQUESTS, row_total, KV_HEADS * 2 * HEAD_DIM)
    return (query, base)


def draw_fresh_q(key, part):
    return fresh_pair(key)[0].astype(jnp.bfloat16)


def draw_fresh_kv(key, part):
    return fresh_pair(key)[1].astype(jnp.bfloat16)


def block_levels(rng, extent, cuts, low, high):
    factor_of = 1.0
    for position, blocks in cuts:
        heights = jax.random.uniform(jax.random.fold_in(jax.random.fold_in(rng, 6), position), (blocks,), jnp.float32, low / len(cuts), high / len(cuts))
        factor_of = factor_of * jnp.repeat(jnp.exp(heights), extent[position] // blocks).reshape((-1,) + (1,) * (len(extent) - 1 - position))
    return factor_of


def scatter_about(rng, shape, scale, most, cuts=(), kind=jnp.bfloat16):
    entries = scale * jax.random.normal(rng, shape, jnp.float32)
    if cuts:
        entries = entries * block_levels(rng, shape, cuts, -0.22, 0.18)
    return jnp.clip(entries, -most, most).astype(kind)


def setup_inputs(seed: int = 0) -> dict:
    seeds = jax.random.split(jax.random.key(seed), 7)
    return {
        "pool_kv": scatter_about(seeds[0], (N_POOL * SLOTS, SPAN_LEN, KV_HEADS * 2 * HEAD_DIM), 1.0, 4.0, ((0, 4), (1, 32))),
        "span_home": draw_span_home(jax.random.fold_in(seeds[6], 71), 0),
        "span_order": draw_span_order(jax.random.fold_in(seeds[6], 71), 0),
        "chosen": draw_chosen(jax.random.fold_in(seeds[6], 71), 0),
        "fresh_q": draw_fresh_q(jax.random.fold_in(seeds[6], 71), 0),
        "fresh_kv": draw_fresh_kv(jax.random.fold_in(seeds[6], 71), 0),
    }


def attend_request(queries, context, places):
    length = context.shape[0]
    split = context.reshape(length, KV_HEADS, 2, HEAD_DIM).astype(jnp.float32)
    keys = split[:, :, 0]
    values = split[:, :, 1]
    grouped = queries.reshape(SELECTED, BLOCK, KV_HEADS, GROUP, HEAD_DIM)
    spots = places.reshape(SELECTED, BLOCK)
    key_pos = jnp.arange(length, dtype=jnp.int32)

    def one_block(pair):
        block_q, block_pos = pair
        scores = jnp.einsum("tkgd,lkd->kgtl", block_q.astype(jnp.float32), keys) * (HEAD_DIM ** -0.5)
        allowed = key_pos[None, None, None, :] <= block_pos[None, None, :, None]
        scores = jnp.where(allowed, scores, -jnp.inf)
        top = jnp.max(scores, axis=-1, keepdims=True)
        weights = jnp.where(allowed, jnp.exp(scores - top), 0.0)
        total = jnp.sum(weights, axis=-1)
        rounded = lax.optimization_barrier(weights.astype(jnp.bfloat16)).astype(jnp.float32)
        mixed = jnp.einsum("kgtl,lkd->tkgd", rounded, values)
        mixed = mixed / jnp.transpose(total, (2, 0, 1))[..., None]
        return mixed.reshape(BLOCK, HEADS * HEAD_DIM).astype(jnp.bfloat16)

    return lax.map(one_block, (grouped, spots)).reshape(SELECTED * BLOCK, HEADS * HEAD_DIM)


def reference(pool_kv, span_home, span_order, chosen, fresh_q, fresh_kv):
    kv_width = pool_kv.shape[-1]
    attended_all = []
    contexts = []
    for request in range(REQUESTS):
        slot_list = span_home[span_order[request]].astype(jnp.int32)
        context = pool_kv[slot_list].reshape(SPANS * SPAN_LEN, kv_width)
        places = (chosen[request][:, None] * BLOCK + jnp.arange(BLOCK, dtype=jnp.int32)[None, :]).reshape(-1).astype(jnp.int32)
        context = context.at[places].set(fresh_kv[request])
        contexts.append(context)
        attended_all.append(attend_request(fresh_q[request], context, places))
    attended = jnp.stack(attended_all)
    stacked = jnp.stack(contexts).reshape(REQUESTS, BLOCKS, N_SEQ, RUN, KV_HEADS, 2 * HEAD_DIM)
    decode_kv = stacked.transpose(4, 2, 0, 1, 3, 5).reshape(KV_HEADS, N_SEQ, REQUESTS, BLOCKS, RUN * 2 * HEAD_DIM)
    return attended, decode_kv
```

```python
import functools
import math

import jax
import jax.numpy as jnp
from jax import lax
from jax.experimental import pallas as pl
from jax.experimental.pallas import tpu as pltpu
from jax.sharding import PartitionSpec as P

MESH = pl.DeviceIdType.MESH
ANY = pl.BlockSpec(memory_space=pl.ANY)
IN_VMEM = pl.BlockSpec(memory_space=pltpu.VMEM)

POOL = 4
HEADS = 4
GROUP = 12
DIM = 128
BLOCK = 128
SPANS = 3
ROWS = 56
PICKED = 14
BLOCKS = 96
WIDE = GROUP * DIM
PAIR = 2 * DIM
CHUNK = 8
STEPS = BLOCKS // CHUNK
KEYS = CHUNK * BLOCK
TILE = 16 * GROUP
LOW = -1e30


def seat(x, z, c):
    return (x * 4 + z) * 2 + c


def here():
    y = lax.axis_index("pool")
    s = lax.axis_index("seq")
    return y, s, s // 8, (s // 2) % 4, s % 2


def remote(src, dst, send, recv, y, s):
    return pltpu.make_async_remote_copy(
        src_ref=src, dst_ref=dst, send_sem=send, recv_sem=recv, device_id=(y, s), device_id_type=MESH
    )


def greet_plane(barrier, y, s):
    def one(d, carry):
        pl.semaphore_signal(barrier, inc=1, device_id=(y, (s + d) % 32), device_id_type=MESH)
        return carry

    lax.fori_loop(1, 32, one, 0)


def pick_kernel(index, src, dst):
    dst[...] = src[...]


def pick_blocks(stack, index, count):
    rows, cols = stack.shape[1:]
    return pl.pallas_call(
        pick_kernel,
        out_shape=jax.ShapeDtypeStruct((count, rows, cols), stack.dtype),
        grid_spec=pltpu.PrefetchScalarGridSpec(
            num_scalar_prefetch=1,
            grid=(count,),
            in_specs=[pl.BlockSpec((1, rows, cols), lambda i, index: (index[i], 0, 0))],
            out_specs=pl.BlockSpec((1, rows, cols), lambda i, index: (i, 0, 0)),
        ),
    )(index, stack)


def first_kernel(out_ref, q_ref, f_ref, arr_ref, qx_ref, fz_ref, hold, y_send, y_recv, q_send, q_recv, f_send, f_recv, l_sem):
    y, s, x, z, c = here()
    barrier = pltpu.get_barrier_semaphore()
    greet_plane(barrier, y, s)
    for d in range(1, POOL):
        pl.semaphore_signal(barrier, inc=1, device_id=((y + d) % POOL, s), device_id_type=MESH)
    own_in = pltpu.make_async_copy(out_ref.at[y], hold, l_sem.at[0])
    own_in.start()
    pl.semaphore_wait(barrier, 31 + POOL - 1)

    passages = []
    for d in (2, 1, 3):
        to = (y + d) % POOL
        copy = remote(out_ref.at[to], arr_ref.at[y], y_send.at[d - 1], y_recv.at[d - 1], to, s)
        copy.start()
        passages.append(copy)
    fresh = []
    for d in (1, 2, 3):
        to = (z + d) % 4
        copy = remote(
            f_ref.at[:, pl.ds(pl.multiple_of(to * PAIR, PAIR), PAIR)],
            fz_ref.at[z],
            f_send.at[d - 1],
            f_recv.at[d - 1],
            y,
            seat(x, to, c),
        )
        copy.start()
        fresh.append(copy)
    own_fresh = pltpu.make_async_copy(
        f_ref.at[:, pl.ds(pl.multiple_of(z * PAIR, PAIR), PAIR)], fz_ref.at[z], l_sem.at[1]
    )
    own_fresh.start()

    def piece(t):
        k, h = t // 4, t % 4
        m = 7 * s + k
        g = m % 8
        to = seat(g // 2, h, g % 2)
        src = q_ref.at[pl.ds(pl.multiple_of(k * 8, 8), 8), pl.ds(pl.multiple_of(h * WIDE, WIDE), WIDE)]
        dst = qx_ref.at[pl.ds(pl.multiple_of((m // 8) * 8, 8), 8), :]
        return src, dst, to

    def send(t, carry):
        src, dst, to = piece(t)

        @pl.when(to != s)
        def _():
            remote(src, dst, q_send.at[t], q_recv, y, to).start()

        @pl.when(to == s)
        def _():
            pltpu.make_async_copy(src, dst, q_recv).start()

        return carry

    lax.fori_loop(0, 28, send, 0)
    own_in.wait()
    own_out = pltpu.make_async_copy(hold, arr_ref.at[y], l_sem.at[0])
    own_out.start()

    def sent(t, carry):
        src, dst, to = piece(t)

        @pl.when(to != s)
        def _():
            remote(src, dst, q_send.at[t], q_recv, y, to).wait_send()

        return carry

    lax.fori_loop(0, 28, sent, 0)
    remote(qx_ref, qx_ref, q_send.at[0], q_recv, y, (s + 1) % 32).wait_recv()
    own_fresh.wait()
    own_out.wait()
    for copy in fresh:
        copy.wait()
    for copy in passages:
        copy.wait()


def first_exchange(outgoing, fresh_q, fresh_kv):
    bf16 = jnp.bfloat16
    dma = pltpu.SemaphoreType.DMA
    return pl.pallas_call(
        first_kernel,
        out_shape=(
            jax.ShapeDtypeStruct((POOL, BLOCK, 1024), bf16),
            jax.ShapeDtypeStruct((4 * ROWS, WIDE), bf16),
            jax.ShapeDtypeStruct((4, ROWS, PAIR), bf16),
        ),
        in_specs=[ANY] * 3,
        out_specs=(ANY,) * 3,
        scratch_shapes=[
            pltpu.VMEM((BLOCK, 1024), bf16),
            dma((3,)),
            dma((3,)),
            dma((28,)),
            dma,
            dma((3,)),
            dma((3,)),
            dma((2,)),
        ],
        compiler_params=pltpu.CompilerParams(collective_id=0, has_side_effects=True),
        name="first_exchange",
    )(outgoing, fresh_q, fresh_kv)


def gather_kernel(kv_ref, fz_ref, all_ref, fr_ref, z_send, z_recv, x_send, x_recv, h_send, h_recv, c_send, c_recv, l_sem):
    y, s, x, z, c = here()
    right, left = (x + 1) % 4, (x + 3) % 4
    far = (x + 2) % 4
    across = seat(x, z, 1 - c)
    barrier = pltpu.get_barrier_semaphore()
    for d in (1, 2, 3):
        pl.semaphore_signal(barrier, inc=1, device_id=(y, seat(x, (z + d) % 4, c)), device_id_type=MESH)
    for to in (seat(right, z, c), seat(left, z, c), across):
        pl.semaphore_signal(barrier, inc=1, device_id=(y, to), device_id_type=MESH)
    pl.semaphore_wait(barrier, 6)

    def head(h):
        return kv_ref.at[:, :, pl.ds(pl.multiple_of(h * PAIR, PAIR), PAIR)]

    shifts = (0, 1, 3, 2)
    pending = []
    z_in = {}
    for d in (1, 3, 2):
        to = (z + d) % 4
        copy = remote(head(to), all_ref.at[x, z, c], z_send.at[d - 1], z_recv.at[d - 1], y, seat(x, to, c))
        copy.start()
        z_in[4 - d] = copy
        pending.append(copy)
    own = pltpu.make_async_copy(head(z), all_ref.at[x, z, c], l_sem.at[0])
    own.start()
    own_fresh = pltpu.make_async_copy(fz_ref, fr_ref.at[x, :, c], l_sem.at[1])
    own_fresh.start()

    def view(p, at, core):
        if p == 0:
            return fr_ref.at[at, :, core]
        return all_ref.at[at, (z + shifts[p - 1]) % 4, core]

    def half(p, at, core, side):
        if p == 0:
            return fr_ref.at[at, pl.ds(2 * side, 2), core]
        return all_ref.at[at, (z + shifts[p - 1]) % 4, core, :, pl.ds(64 * side, 64)]

    def ring(p, way):
        to = right if way == 0 else left
        return remote(view(p, x, c), view(p, x, c), x_send.at[way, p], x_recv.at[way, p], y, seat(to, z, c))

    def ring_in(p, way):
        at = left if way == 0 else right
        return remote(view(p, at, c), view(p, at, c), x_send.at[way, p], x_recv.at[way, p], y, seat(at, z, c))

    def onward(p, way):
        at, to = (left, right) if way == 0 else (right, left)
        return remote(half(p, at, c, way), half(p, at, c, way), h_send.at[way, p], h_recv.at[way, p], y, seat(to, z, c))

    def onward_in(p, way):
        return remote(half(p, far, c, way), half(p, far, c, way), h_send.at[way, p], h_recv.at[way, p], y, seat(left, z, c))

    def give(p, kind, core):
        if kind < 3:
            v = view(p, (x, left, right)[kind], core)
        else:
            v = half(p, far, core, kind - 3)
        return remote(v, v, c_send.at[kind, p], c_recv.at[kind, p], y, across)

    def start(copy):
        copy.start()
        pending.append(copy)

    def own_ready(p):
        if p == 0:
            own_fresh.wait()
        elif p == 1:
            own.wait()
        else:
            z_in[shifts[p - 1]].wait_recv()
        start(ring(p, 0))
        start(ring(p, 1))
        start(give(p, 0, c))

    def passed(p):
        for way in (0, 1):
            ring_in(p, way).wait_recv()
            start(onward(p, way))
            start(give(p, 1 + way, c))

    for p in range(5):
        own_ready(p)
    for p in range(5):
        passed(p)
    for p in range(5):
        for way in (0, 1):
            onward_in(p, way).wait_recv()
            start(give(p, 3 + way, c))
    for p in range(5):
        for kind in range(5):
            give(p, kind, 1 - c).wait_recv()
    for copy in pending:
        copy.wait_send()


def gather_head(cached, fz):
    bf16 = jnp.bfloat16
    dma = pltpu.SemaphoreType.DMA
    return pl.pallas_call(
        gather_kernel,
        out_shape=(
            jax.ShapeDtypeStruct((4, 4, 2, SPANS, BLOCK, PAIR), bf16),
            jax.ShapeDtypeStruct((4, 4, 2, ROWS, PAIR), bf16),
        ),
        in_specs=[IN_VMEM, IN_VMEM],
        out_specs=(ANY, ANY),
        scratch_shapes=[
            dma((3,)),
            dma((3,)),
            dma((2, 5)),
            dma((2, 5)),
            dma((2, 5)),
            dma((2, 5)),
            dma((5, 5)),
            dma((5, 5)),
            dma((2,)),
        ],
        compiler_params=pltpu.CompilerParams(collective_id=1, has_side_effects=True),
        name="gather_head",
    )(cached, fz)


def attend_kernel(chosen, group, kv_ref, fr_ref, qx_ref, att_ref, dec_ref, kv, fresh, q, top, acc, rows32, sems):
    g = group[0]
    bf16, f32 = jnp.bfloat16, jnp.float32

    def load(step):
        j, part = step // 4, step % 4
        return pltpu.make_async_copy(
            kv_ref.at[pl.ds(part * CHUNK, CHUNK), j], kv.at[pl.ds(step * CHUNK, CHUNK)], sems.at[step]
        )

    fresh_in = pltpu.make_async_copy(fr_ref, fresh, sems.at[STEPS])
    fresh_in.start()
    for step in range(STEPS):
        load(step).start()

    scale = math.log2(math.e) / math.sqrt(DIM)

    def prepare(i, carry):
        r0 = pl.multiple_of(i * 16, 16)
        for hd in range(GROUP):
            full = qx_ref[pl.ds(r0, 16), hd * DIM : (hd + 1) * DIM].astype(f32) * scale
            q[i, hd * 16 : (hd + 1) * 16, 0:DIM] = full.astype(bf16)
            high = q[i, hd * 16 : (hd + 1) * 16, 0:DIM].astype(f32)
            q[i, hd * 16 : (hd + 1) * 16, DIM:PAIR] = (full - high).astype(bf16)
        top[i] = jnp.full((TILE, DIM), LOW, f32)
        acc[i] = jnp.zeros((TILE, PAIR), f32)
        return carry

    lax.fori_loop(0, PICKED, prepare, 0)
    fresh_in.wait()

    def before(block):
        total = jnp.int32(0)
        for i in range(PICKED):
            total = total + jnp.where(chosen[i] < block, 1, 0).astype(jnp.int32)
        return total

    ones = jnp.ones((KEYS, DIM), bf16)

    def fold(i, n, keys, values, mask_from):
        qq = q[pl.ds(i, n)].reshape(n * TILE, PAIR)
        s = lax.dot_general(qq, keys, (((1,), (1,)), ((), ())), preferred_element_type=f32)
        if mask_from is not None:
            row = lax.broadcasted_iota(jnp.int32, (TILE, KEYS), 0)
            token = 64 * ((row % 16) // 8) + 8 * g + row % 8
            key = lax.broadcasted_iota(jnp.int32, (TILE, KEYS), 1)
            s = jnp.where(key <= token + mask_from, s, LOW)
        old = top[pl.ds(i, n)].reshape(n * TILE, DIM)
        new = jnp.maximum(old, jnp.max(s, axis=1, keepdims=True))
        w = jnp.exp2(s - new[:, 0:1]).astype(bf16)
        part = jnp.dot(w, values, preferred_element_type=f32)
        factor = jnp.exp2(old - new)
        both = jnp.concatenate([factor, factor], axis=1)
        acc[pl.ds(i, n)] = (acc[pl.ds(i, n)].reshape(n * TILE, PAIR) * both + part).reshape(n, TILE, PAIR)
        top[pl.ds(i, n)] = new.reshape(n, TILE, DIM)

    def step_body(step, first):
        load(step).wait()
        last = before((step + 1) * CHUNK)

        def patch(i, carry):
            kv[chosen[i]] = fresh[pl.ds(pl.multiple_of(i * BLOCK, BLOCK), BLOCK), :]
            return carry

        lax.fori_loop(first, last, patch, 0)

        at = step * CHUNK
        slab = kv[pl.ds(at, CHUNK), pl.ds(pl.multiple_of(g * 16, 16), 16), :].astype(f32)
        flat = slab.reshape(CHUNK * 16, PAIR)
        for side in range(2):
            rows32[side] = flat[:, side * DIM : (side + 1) * DIM]
        for k in range(4):
            for u in range(4):
                for side in range(2):
                    line = rows32[side, pl.ds(4 * k + u, CHUNK, stride=16), :]
                    to = u * PAIR + side * DIM
                    dec_ref[k, pl.ds(pl.multiple_of(at, CHUNK), CHUNK), to : to + DIM] = line.astype(bf16)

        both = kv[pl.ds(at, CHUNK)].reshape(KEYS, PAIR)
        keys = jnp.concatenate([both[:, :DIM], both[:, :DIM]], axis=1)
        values = jnp.concatenate([both[:, DIM:], ones], axis=1)

        def diagonal(i, carry):
            fold(i, 1, keys, values, (chosen[i] - at) * BLOCK)
            return carry

        lax.fori_loop(first, last, diagonal, 0)
        left = PICKED - last
        odd = left % 2

        @pl.when(odd == 1)
        def _():
            fold(last, 1, keys, values, None)

        def two(t, carry):
            fold(last + odd + 2 * t, 2, keys, values, None)
            return carry

        lax.fori_loop(0, left // 2, two, 0)
        return last

    lax.fori_loop(0, STEPS, step_body, jnp.int32(0))

    def finish(i, carry):
        out = acc[i, :, 0:DIM] / acc[i, :, DIM:PAIR]
        r0 = pl.multiple_of(i * 16, 16)
        for hd in range(GROUP):
            att_ref[pl.ds(r0, 16), hd * DIM : (hd + 1) * DIM] = out[hd * 16 : (hd + 1) * 16].astype(bf16)
        return carry

    lax.fori_loop(0, PICKED, finish, 0)


def attend(chosen, group, kv, fresh, qx):
    bf16, f32 = jnp.bfloat16, jnp.float32
    smem = pl.BlockSpec(memory_space=pltpu.SMEM)
    return pl.pallas_call(
        attend_kernel,
        out_shape=(
            jax.ShapeDtypeStruct((4 * ROWS, WIDE), bf16),
            jax.ShapeDtypeStruct((4, BLOCKS, 1024), bf16),
        ),
        in_specs=[smem, smem, ANY, ANY, IN_VMEM],
        out_specs=(IN_VMEM, IN_VMEM),
        scratch_shapes=[
            pltpu.VMEM((BLOCKS, BLOCK, PAIR), bf16),
            pltpu.VMEM((PICKED * BLOCK, PAIR), bf16),
            pltpu.VMEM((PICKED, TILE, PAIR), bf16),
            pltpu.VMEM((PICKED, TILE, DIM), f32),
            pltpu.VMEM((PICKED, TILE, PAIR), f32),
            pltpu.VMEM((2, CHUNK * 16, DIM), f32),
            pltpu.SemaphoreType.DMA((STEPS + 1,)),
        ],
        compiler_params=pltpu.CompilerParams(vmem_limit_bytes=48 * 1024 * 1024),
        name="attend",
    )(chosen, group, kv, fresh, qx)


def last_kernel(att_ref, dec_ref, out_ref, laid_ref, a_send, a_recv, d_send, d_recv):
    y, s, x, z, c = here()
    g = 2 * x + c
    barrier = pltpu.get_barrier_semaphore()
    greet_plane(barrier, y, s)
    giver = s // 4
    for d in range(1, POOL):
        source = seat(giver // 2, y, giver % 2)
        pl.semaphore_signal(barrier, inc=1, device_id=((y + d) % POOL, source), device_id_type=MESH)
    pl.semaphore_wait(barrier, 31 + jnp.where(z == y, 0, 4))

    def slab(k):
        return dec_ref.at[k], laid_ref.at[y], 4 * g + k

    def slab_send(k, carry):
        src, dst, to = slab(k)
        mine = jnp.logical_and(z == y, to == s)

        @pl.when(jnp.logical_not(mine))
        def _():
            remote(src, dst, d_send.at[k], d_recv, z, to).start()

        @pl.when(mine)
        def _():
            pltpu.make_async_copy(src, dst, d_recv).start()

        return carry

    lax.fori_loop(0, 4, slab_send, 0)

    def piece(j):
        m = 8 * j + g
        src = att_ref.at[pl.ds(pl.multiple_of(j * 8, 8), 8), :]
        dst = out_ref.at[
            pl.ds(pl.multiple_of((m % 7) * 8, 8), 8), pl.ds(pl.multiple_of(z * WIDE, WIDE), WIDE)
        ]
        return src, dst, m // 7

    def send(j, carry):
        src, dst, to = piece(j)

        @pl.when(to != s)
        def _():
            remote(src, dst, a_send.at[j], a_recv, y, to).start()

        @pl.when(to == s)
        def _():
            pltpu.make_async_copy(src, dst, a_recv).start()

        return carry

    lax.fori_loop(0, 28, send, 0)

    def slab_sent(k, carry):
        src, dst, to = slab(k)
        mine = jnp.logical_and(z == y, to == s)

        @pl.when(jnp.logical_not(mine))
        def _():
            remote(src, dst, d_send.at[k], d_recv, z, to).wait_send()

        return carry

    lax.fori_loop(0, 4, slab_sent, 0)

    def sent(j, carry):
        src, dst, to = piece(j)

        @pl.when(to != s)
        def _():
            remote(src, dst, a_send.at[j], a_recv, y, to).wait_send()

        return carry

    lax.fori_loop(0, 28, sent, 0)
    remote(out_ref, out_ref, a_send.at[0], a_recv, y, (s + 1) % 32).wait_recv()
    remote(laid_ref, laid_ref, d_send.at[0], d_recv, y, (s + 1) % 32).wait_recv()


def last_exchange(att, dec):
    bf16 = jnp.bfloat16
    dma = pltpu.SemaphoreType.DMA
    return pl.pallas_call(
        last_kernel,
        out_shape=(
            jax.ShapeDtypeStruct((ROWS, HEADS * WIDE), bf16),
            jax.ShapeDtypeStruct((POOL, BLOCKS, 1024), bf16),
        ),
        in_specs=[ANY, ANY],
        out_specs=(ANY, ANY),
        scratch_shapes=[dma((28,)), dma, dma((4,)), dma],
        compiler_params=pltpu.CompilerParams(collective_id=2, has_side_effects=True),
        name="last_exchange",
    )(att, dec)


def shards(pool_kv, span_home, span_order, chosen, fresh_q, fresh_kv):
    replica = lax.axis_index("pool")
    my_seat = lax.axis_index("seq")
    home_replica = span_home // 4
    home_slot = span_home % 4
    held = jnp.where(home_replica == replica, home_slot, 0).reshape(POOL, SPANS)
    outgoing = pick_blocks(pool_kv, jnp.sum(held, axis=1).astype(jnp.int32), POOL)
    arrived, qx, fz = first_exchange(outgoing, fresh_q[0], fresh_kv[0])
    lookup = span_order[0][:, None] == jnp.arange(POOL * SPANS, dtype=jnp.int32)[None, :]
    source = jnp.sum(jnp.where(lookup, home_replica[None, :], 0), axis=1).astype(jnp.int32)
    cached = pick_blocks(arrived, source, SPANS)
    kv, fresh = gather_head(cached, fz)
    group = (2 * (my_seat // 8) + my_seat % 2).astype(jnp.int32).reshape(1)
    att, dec = attend(
        chosen[0], group, kv.reshape(32, SPANS, BLOCK, PAIR), fresh.reshape(32 * ROWS, PAIR), qx
    )
    attended, laid = last_exchange(att, dec)
    return attended[None], laid[None, None]


def solution(mesh):
    in_specs = (
        P("pool", "seq", None),
        P(),
        P("pool", None),
        P("pool", None),
        P("pool", "seq", None),
        P("pool", "seq", None),
    )
    out_specs = (P("pool", "seq", None), P("pool", "seq", None, None, None))
    return jax.shard_map(shards, mesh=mesh, in_specs=in_specs, out_specs=out_specs, check_vma=False)
```

```python
import functools
import math

import jax
import jax.numpy as jnp
from jax import lax
from jax.experimental import pallas as pl
from jax.experimental.pallas import tpu as pltpu
from jax.sharding import PartitionSpec as P

MESH = pl.DeviceIdType.MESH
ANY = pl.BlockSpec(memory_space=pl.ANY)
IN_VMEM = pl.BlockSpec(memory_space=pltpu.VMEM)

POOL = 4
HEADS = 4
GROUP = 12
DIM = 128
BLOCK = 128
SPANS = 3
ROWS = 56
PICKED = 14
BLOCKS = 96
WIDE = GROUP * DIM
PAIR = 2 * DIM
CHUNK = 8
STEPS = BLOCKS // CHUNK
KEYS = CHUNK * BLOCK
TILE = 16 * GROUP
PAIRS = PICKED // 2
ITEM = 2 * TILE
STRIP = 32
LOW = -1e30


def seat(x, z, c):
    return (x * 4 + z) * 2 + c


def here():
    y = lax.axis_index("pool")
    s = lax.axis_index("seq")
    return y, s, s // 8, (s // 2) % 4, s % 2


def remote(src, dst, send, recv, y, s):
    return pltpu.make_async_remote_copy(
        src_ref=src, dst_ref=dst, send_sem=send, recv_sem=recv, device_id=(y, s), device_id_type=MESH
    )


def greet_plane(barrier, y, s):
    def one(d, carry):
        pl.semaphore_signal(barrier, inc=1, device_id=(y, (s + d) % 32), device_id_type=MESH)
        return carry

    lax.fori_loop(1, 32, one, 0)


def pick_kernel(index, src, dst):
    dst[...] = src[...]


def pick_blocks(stack, index, count):
    rows, cols = stack.shape[1:]
    return pl.pallas_call(
        pick_kernel,
        out_shape=jax.ShapeDtypeStruct((count, rows, cols), stack.dtype),
        grid_spec=pltpu.PrefetchScalarGridSpec(
            num_scalar_prefetch=1,
            grid=(count,),
            in_specs=[pl.BlockSpec((1, rows, cols), lambda i, index: (index[i], 0, 0))],
            out_specs=pl.BlockSpec((1, rows, cols), lambda i, index: (i, 0, 0)),
        ),
    )(index, stack)


def first_kernel(out_ref, q_ref, f_ref, arr_ref, qx_ref, fz_ref, hold, y_send, y_recv, q_send, q_recv, f_send, f_recv, l_sem):
    y, s, x, z, c = here()
    barrier = pltpu.get_barrier_semaphore()
    greet_plane(barrier, y, s)
    for d in range(1, POOL):
        pl.semaphore_signal(barrier, inc=1, device_id=((y + d) % POOL, s), device_id_type=MESH)
    own_in = pltpu.make_async_copy(out_ref.at[y], hold, l_sem.at[0])
    own_in.start()
    pl.semaphore_wait(barrier, 31 + POOL - 1)

    passages = []
    for d in (2, 1, 3):
        to = (y + d) % POOL
        copy = remote(out_ref.at[to], arr_ref.at[y], y_send.at[d - 1], y_recv.at[d - 1], to, s)
        copy.start()
        passages.append(copy)
    fresh = []
    for d in (1, 2, 3):
        to = (z + d) % 4
        copy = remote(
            f_ref.at[:, pl.ds(pl.multiple_of(to * PAIR, PAIR), PAIR)],
            fz_ref.at[z],
            f_send.at[d - 1],
            f_recv.at[d - 1],
            y,
            seat(x, to, c),
        )
        copy.start()
        fresh.append(copy)
    own_fresh = pltpu.make_async_copy(
        f_ref.at[:, pl.ds(pl.multiple_of(z * PAIR, PAIR), PAIR)], fz_ref.at[z], l_sem.at[1]
    )
    own_fresh.start()

    def piece(t):
        k, h = t // 4, t % 4
        m = 7 * s + k
        g = m % 8
        to = seat(g // 2, h, g % 2)
        src = q_ref.at[pl.ds(pl.multiple_of(k * 8, 8), 8), pl.ds(pl.multiple_of(h * WIDE, WIDE), WIDE)]
        dst = qx_ref.at[pl.ds(pl.multiple_of((m // 8) * 8, 8), 8), :]
        return src, dst, to

    def send(t, carry):
        src, dst, to = piece(t)

        @pl.when(to != s)
        def _():
            remote(src, dst, q_send.at[t], q_recv, y, to).start()

        @pl.when(to == s)
        def _():
            pltpu.make_async_copy(src, dst, q_recv).start()

        return carry

    lax.fori_loop(0, 28, send, 0)
    own_in.wait()
    own_out = pltpu.make_async_copy(hold, arr_ref.at[y], l_sem.at[0])
    own_out.start()

    def sent(t, carry):
        src, dst, to = piece(t)

        @pl.when(to != s)
        def _():
            remote(src, dst, q_send.at[t], q_recv, y, to).wait_send()

        return carry

    lax.fori_loop(0, 28, sent, 0)
    remote(qx_ref, qx_ref, q_send.at[0], q_recv, y, (s + 1) % 32).wait_recv()
    own_fresh.wait()
    own_out.wait()
    for copy in fresh:
        copy.wait()
    for copy in passages:
        copy.wait()


def first_exchange(outgoing, fresh_q, fresh_kv):
    bf16 = jnp.bfloat16
    dma = pltpu.SemaphoreType.DMA
    return pl.pallas_call(
        first_kernel,
        out_shape=(
            jax.ShapeDtypeStruct((POOL, BLOCK, 1024), bf16),
            jax.ShapeDtypeStruct((4 * ROWS, WIDE), bf16),
            jax.ShapeDtypeStruct((4, ROWS, PAIR), bf16),
        ),
        in_specs=[ANY] * 3,
        out_specs=(ANY,) * 3,
        scratch_shapes=[
            pltpu.VMEM((BLOCK, 1024), bf16),
            dma((3,)),
            dma((3,)),
            dma((28,)),
            dma,
            dma((3,)),
            dma((3,)),
            dma((2,)),
        ],
        compiler_params=pltpu.CompilerParams(collective_id=0, has_side_effects=True),
        name="first_exchange",
    )(outgoing, fresh_q, fresh_kv)


def gather_kernel(kv_ref, fz_ref, all_ref, fr_ref, z_send, z_recv, x_send, x_recv, h_send, h_recv, c_send, c_recv, l_sem):
    y, s, x, z, c = here()
    right, left = (x + 1) % 4, (x + 3) % 4
    far = (x + 2) % 4
    across = seat(x, z, 1 - c)
    barrier = pltpu.get_barrier_semaphore()
    for d in (1, 2, 3):
        pl.semaphore_signal(barrier, inc=1, device_id=(y, seat(x, (z + d) % 4, c)), device_id_type=MESH)
    for to in (seat(right, z, c), seat(left, z, c), across):
        pl.semaphore_signal(barrier, inc=1, device_id=(y, to), device_id_type=MESH)
    pl.semaphore_wait(barrier, 6)

    def head(h):
        return kv_ref.at[:, :, pl.ds(pl.multiple_of(h * PAIR, PAIR), PAIR)]

    shifts = (0, 1, 3, 2)
    pending = []
    z_in = {}
    for d in (1, 3, 2):
        to = (z + d) % 4
        copy = remote(head(to), all_ref.at[x, z, c], z_send.at[d - 1], z_recv.at[d - 1], y, seat(x, to, c))
        copy.start()
        z_in[4 - d] = copy
        pending.append(copy)
    own = pltpu.make_async_copy(head(z), all_ref.at[x, z, c], l_sem.at[0])
    own.start()
    own_fresh = pltpu.make_async_copy(fz_ref, fr_ref.at[x, :, c], l_sem.at[1])
    own_fresh.start()

    def view(p, at, core):
        if p == 0:
            return fr_ref.at[at, :, core]
        return all_ref.at[at, (z + shifts[p - 1]) % 4, core]

    def half(p, at, core, side):
        if p == 0:
            return fr_ref.at[at, pl.ds(2 * side, 2), core]
        return all_ref.at[at, (z + shifts[p - 1]) % 4, core, :, pl.ds(64 * side, 64)]

    def ring(p, way):
        to = right if way == 0 else left
        return remote(view(p, x, c), view(p, x, c), x_send.at[way, p], x_recv.at[way, p], y, seat(to, z, c))

    def ring_in(p, way):
        at = left if way == 0 else right
        return remote(view(p, at, c), view(p, at, c), x_send.at[way, p], x_recv.at[way, p], y, seat(at, z, c))

    def onward(p, way):
        at, to = (left, right) if way == 0 else (right, left)
        return remote(half(p, at, c, way), half(p, at, c, way), h_send.at[way, p], h_recv.at[way, p], y, seat(to, z, c))

    def onward_in(p, way):
        return remote(half(p, far, c, way), half(p, far, c, way), h_send.at[way, p], h_recv.at[way, p], y, seat(left, z, c))

    def give(p, kind, core):
        if kind < 3:
            v = view(p, (x, left, right)[kind], core)
        else:
            v = half(p, far, core, kind - 3)
        return remote(v, v, c_send.at[kind, p], c_recv.at[kind, p], y, across)

    def start(copy):
        copy.start()
        pending.append(copy)

    def own_ready(p):
        if p == 0:
            own_fresh.wait()
        elif p == 1:
            own.wait()
        else:
            z_in[shifts[p - 1]].wait_recv()
        start(ring(p, 0))
        start(ring(p, 1))
        start(give(p, 0, c))

    def passed(p):
        for way in (0, 1):
            ring_in(p, way).wait_recv()
            start(onward(p, way))
            start(give(p, 1 + way, c))

    for p in range(5):
        own_ready(p)
    for p in range(5):
        passed(p)
    for p in range(5):
        for way in (0, 1):
            onward_in(p, way).wait_recv()
            start(give(p, 3 + way, c))
    for p in range(5):
        for kind in range(5):
            give(p, kind, 1 - c).wait_recv()
    for copy in pending:
        copy.wait_send()


def gather_head(cached, fz):
    bf16 = jnp.bfloat16
    dma = pltpu.SemaphoreType.DMA
    return pl.pallas_call(
        gather_kernel,
        out_shape=(
            jax.ShapeDtypeStruct((4, 4, 2, SPANS, BLOCK, PAIR), bf16),
            jax.ShapeDtypeStruct((4, 4, 2, ROWS, PAIR), bf16),
        ),
        in_specs=[IN_VMEM, IN_VMEM],
        out_specs=(ANY, ANY),
        scratch_shapes=[
            dma((3,)),
            dma((3,)),
            dma((2, 5)),
            dma((2, 5)),
            dma((2, 5)),
            dma((2, 5)),
            dma((5, 5)),
            dma((5, 5)),
            dma((2,)),
        ],
        compiler_params=pltpu.CompilerParams(collective_id=1, has_side_effects=True),
        name="gather_head",
    )(cached, fz)


def attend_kernel(
    chosen, group, kv_ref, fr_ref, qx_ref, att_ref, dec_ref,
    kv, fresh, q, top, acc, s_a, s_b, w_a, w_b, f_a, f_b, rows32, sems,
):
    g = group[0]
    bf16, f32 = jnp.bfloat16, jnp.float32

    def load(step):
        j, part = step // 4, step % 4
        for side in range(2):
            yield pltpu.make_async_copy(
                kv_ref.at[pl.ds(part * CHUNK, CHUNK), j, :, pl.ds(side * DIM, DIM)],
                kv.at[side, pl.ds(step * CHUNK, CHUNK)],
                sems.at[side, step],
            )

    fresh_in = [
        pltpu.make_async_copy(fr_ref.at[:, pl.ds(side * DIM, DIM)], fresh.at[side], sems.at[side, STEPS])
        for side in range(2)
    ]
    for copy in fresh_in:
        copy.start()
    for step in range(STEPS):
        for copy in load(step):
            copy.start()

    scale = math.log2(math.e) / math.sqrt(DIM)

    def prepare(i, carry):
        r0 = pl.multiple_of(i * 16, 16)
        half = (i % 2) * TILE
        for hd in range(GROUP):
            to = pl.multiple_of(half + hd * 16, 16)
            q[i // 2, pl.ds(to, 16), :] = qx_ref[pl.ds(r0, 16), hd * DIM : (hd + 1) * DIM]
        return carry

    lax.fori_loop(0, PICKED, prepare, 0)

    def clear(p, carry):
        top[p] = jnp.full((ITEM, DIM), LOW, f32)
        acc[p] = jnp.zeros((ITEM, PAIR), f32)
        return carry

    lax.fori_loop(0, PAIRS, clear, 0)
    w_b[...] = jnp.zeros((CHUNK, ITEM, DIM), bf16)
    f_b[...] = jnp.ones((ITEM, DIM), f32)
    for copy in fresh_in:
        copy.wait()

    def before(block):
        total = jnp.int32(0)
        for i in range(PICKED):
            total = total + jnp.where(chosen[i] < block, 1, 0).astype(jnp.int32)
        return total

    def make_ready(step):
        for copy in load(step):
            copy.wait()

        def patch(i, carry):
            for side in range(2):
                kv[side, chosen[i]] = fresh[side, pl.ds(pl.multiple_of(i * BLOCK, BLOCK), BLOCK), :]
            return carry

        lax.fori_loop(before(step * CHUNK), before((step + 1) * CHUNK), patch, 0)
        at = step * CHUNK
        for side in range(2):
            slab = kv[side, pl.ds(at, CHUNK), pl.ds(pl.multiple_of(g * 16, 16), 16), :].astype(f32)
            rows32[side] = slab.reshape(CHUNK * 16, DIM)
        for k in range(4):
            for u in range(4):
                for side in range(2):
                    line = rows32[side, pl.ds(4 * k + u, CHUNK, stride=16), :]
                    to = u * PAIR + side * DIM
                    dec_ref[k, pl.ds(pl.multiple_of(at, CHUNK), CHUNK), to : to + DIM] = line.astype(bf16)

    ones = jnp.ones((KEYS, DIM), bf16)

    def scores(p, step, s):
        keys = kv[0, pl.ds(step * CHUNK, CHUNK)].reshape(KEYS, DIM)
        s[...] = lax.dot_general(q[p], keys, (((1,), (1,)), ((), ())), preferred_element_type=f32)

    def hide(p, step, s, dead):
        for side in range(2):
            rows = slice(side * TILE, (side + 1) * TILE)
            own = jnp.where(dead, -1, chosen[2 * p + side] - step * CHUNK)

            def blank(j, carry):
                s[rows, pl.ds(pl.multiple_of(j * BLOCK, BLOCK), BLOCK)] = jnp.full((TILE, BLOCK), LOW, f32)
                return carry

            lax.fori_loop(jnp.clip(own + 1, 0, CHUNK), CHUNK, blank, 0)

            @pl.when(jnp.logical_and(own >= 0, own < CHUNK))
            def _():
                cols = pl.ds(pl.multiple_of(own * BLOCK, BLOCK), BLOCK)
                row = lax.broadcasted_iota(jnp.int32, (TILE, BLOCK), 0)
                token = 64 * ((row % 16) // 8) + 8 * g + row % 8
                key = lax.broadcasted_iota(jnp.int32, (TILE, BLOCK), 1)
                s[rows, cols] = jnp.where(key <= token, s[rows, cols], LOW)

    def soften(p, s, w, f, lo, hi):
        for r in range(lo, hi, STRIP):
            rows = slice(r, r + STRIP)
            parts = [s[rows, j * DIM : (j + 1) * DIM] for j in range(CHUNK)]
            best = functools.reduce(jnp.maximum, parts)
            old = top[p, rows, :]
            new = jnp.maximum(old, jnp.max(best, axis=1, keepdims=True))
            for j in range(CHUNK):
                w[j, rows, :] = jnp.exp2((parts[j] - new) * scale).astype(bf16)
            f[rows, :] = jnp.exp2((old - new) * scale)
            top[p, rows, :] = new

    def mix(p, step, w, f, lo, hi):
        values = jnp.concatenate([kv[1, pl.ds(step * CHUNK, CHUNK)].reshape(KEYS, DIM), ones], axis=1)
        weights = jnp.concatenate([w[j, lo:hi, :] for j in range(CHUNK)], axis=1)
        part = jnp.dot(weights, values, preferred_element_type=f32)
        factor = f[lo:hi, :]
        acc[p, lo:hi, :] = acc[p, lo:hi, :] * jnp.concatenate([factor, factor], axis=1) + part

    def last_of(p):
        return chosen[2 * p + 1] // CHUNK

    total = jnp.int32(0)
    for p in range(PAIRS):
        total = total + last_of(p) + 1

    def following(item):
        p, step = item
        more = step < last_of(p)
        return (
            jnp.where(more, p, jnp.minimum(p + 1, PAIRS - 1)),
            jnp.where(more, step + 1, 0),
        )

    def turn(t, ready, last, now, s_now, s_next, w_now, w_last, f_now, f_last):
        after = following(now)
        fits = after[1] < ready

        @pl.when(jnp.logical_not(fits))
        def _():
            make_ready(after[1])

        dead = t >= total
        @pl.when(jnp.logical_or(dead, chosen[2 * now[0]] < (now[1] + 1) * CHUNK))
        def _():
            hide(now[0], now[1], s_now, dead)

        scores(after[0], after[1], s_next)
        for lo in range(0, ITEM, TILE):
            soften(now[0], s_now, w_now, f_now, lo, lo + TILE)
            mix(now[0], now[1], w_now, f_now, lo, lo + TILE)
        return jnp.where(fits, ready, after[1] + 1), now, after

    def both_turns(i, carry):
        ready, last, now = carry
        ready, last, now = turn(2 * i, ready, last, now, s_a, s_b, w_a, w_b, f_a, f_b)
        ready, last, now = turn(2 * i + 1, ready, last, now, s_b, s_a, w_b, w_a, f_b, f_a)
        return ready, last, now

    make_ready(0)
    zero = jnp.int32(0)
    scores(0, 0, s_a)
    ready, last, now = lax.fori_loop(0, (total + 1) // 2, both_turns, (jnp.int32(1), (zero, zero), (zero, zero)))

    def rest(step, carry):
        make_ready(step)
        return carry

    lax.fori_loop(ready, STEPS, rest, 0)

    def finish(i, carry):
        half = (i % 2) * TILE
        r0 = pl.multiple_of(i * 16, 16)
        for hd in range(GROUP):
            rows = pl.ds(pl.multiple_of(half + hd * 16, 16), 16)
            out = acc[i // 2, rows, 0:DIM] / acc[i // 2, rows, DIM:PAIR]
            att_ref[pl.ds(r0, 16), hd * DIM : (hd + 1) * DIM] = out.astype(bf16)
        return carry

    lax.fori_loop(0, PICKED, finish, 0)


def attend(chosen, group, kv, fresh, qx):
    bf16, f32 = jnp.bfloat16, jnp.float32
    smem = pl.BlockSpec(memory_space=pltpu.SMEM)
    return pl.pallas_call(
        attend_kernel,
        out_shape=(
            jax.ShapeDtypeStruct((4 * ROWS, WIDE), bf16),
            jax.ShapeDtypeStruct((4, BLOCKS, 1024), bf16),
        ),
        in_specs=[smem, smem, ANY, ANY, IN_VMEM],
        out_specs=(IN_VMEM, IN_VMEM),
        scratch_shapes=[
            pltpu.VMEM((2, BLOCKS, BLOCK, DIM), bf16),
            pltpu.VMEM((2, PICKED * BLOCK, DIM), bf16),
            pltpu.VMEM((PAIRS, ITEM, DIM), bf16),
            pltpu.VMEM((PAIRS, ITEM, DIM), f32),
            pltpu.VMEM((PAIRS, ITEM, PAIR), f32),
            pltpu.VMEM((ITEM, KEYS), f32),
            pltpu.VMEM((ITEM, KEYS), f32),
            pltpu.VMEM((CHUNK, ITEM, DIM), bf16),
            pltpu.VMEM((CHUNK, ITEM, DIM), bf16),
            pltpu.VMEM((ITEM, DIM), f32),
            pltpu.VMEM((ITEM, DIM), f32),
            pltpu.VMEM((2, CHUNK * 16, DIM), f32),
            pltpu.SemaphoreType.DMA((2, STEPS + 1)),
        ],
        compiler_params=pltpu.CompilerParams(vmem_limit_bytes=58 * 1024 * 1024),
        name="attend",
    )(chosen, group, kv, fresh, qx)


def last_kernel(
    att_ref, dec_ref, out_ref, laid_ref, mid, a_send, a_recv, z_send, z_recv, y_send, y_recv
):
    y, s, x, z, c = here()
    g = 2 * x + c
    barrier = pltpu.get_barrier_semaphore()
    greet_plane(barrier, y, s)
    for d in range(1, POOL):
        pl.semaphore_signal(barrier, inc=1, device_id=((y + d) % POOL, s), device_id_type=MESH)
    pl.semaphore_wait(barrier, 31 + POOL - 1)

    def slab(k):
        to_z, to_c = 2 * c + k // 2, k % 2
        return dec_ref.at[k], mid.at[z], seat(x, to_z, to_c)

    def slab_send(k, carry):
        src, dst, to = slab(k)

        @pl.when(to != s)
        def _():
            remote(src, dst, z_send.at[k], z_recv.at[z], y, to).start()

        @pl.when(to == s)
        def _():
            pltpu.make_async_copy(src, dst, z_recv.at[z]).start()

        return carry

    lax.fori_loop(0, 4, slab_send, 0)

    def piece(j):
        m = 8 * j + g
        src = att_ref.at[pl.ds(pl.multiple_of(j * 8, 8), 8), :]
        dst = out_ref.at[
            pl.ds(pl.multiple_of((m % 7) * 8, 8), 8), pl.ds(pl.multiple_of(z * WIDE, WIDE), WIDE)
        ]
        return src, dst, m // 7

    def send(j, carry):
        src, dst, to = piece(j)

        @pl.when(to != s)
        def _():
            remote(src, dst, a_send.at[j], a_recv, y, to).start()

        @pl.when(to == s)
        def _():
            pltpu.make_async_copy(src, dst, a_recv).start()

        return carry

    lax.fori_loop(0, 28, send, 0)

    passing = []
    for d in (0, 1, 3, 2):
        h = (z + d) % 4
        remote(mid.at[h], mid.at[h], y_send.at[d], z_recv.at[h], y, (s + 1) % 32).wait_recv()
        copy = remote(mid.at[h], laid_ref.at[y], y_send.at[d], y_recv, h, s)
        own = pltpu.make_async_copy(mid.at[h], laid_ref.at[y], y_recv)

        @pl.when(h != y)
        def _():
            copy.start()

        @pl.when(h == y)
        def _():
            own.start()

        passing.append((h, copy))

    def slab_sent(k, carry):
        src, dst, to = slab(k)

        @pl.when(to != s)
        def _():
            remote(src, dst, z_send.at[k], z_recv.at[z], y, to).wait_send()

        return carry

    lax.fori_loop(0, 4, slab_sent, 0)

    def sent(j, carry):
        src, dst, to = piece(j)

        @pl.when(to != s)
        def _():
            remote(src, dst, a_send.at[j], a_recv, y, to).wait_send()

        return carry

    lax.fori_loop(0, 28, sent, 0)
    for h, copy in passing:

        @pl.when(h != y)
        def _():
            copy.wait_send()

    remote(out_ref, out_ref, a_send.at[0], a_recv, y, (s + 1) % 32).wait_recv()
    remote(laid_ref, laid_ref, y_send.at[0], y_recv, y, (s + 1) % 32).wait_recv()


def last_exchange(att, dec):
    bf16 = jnp.bfloat16
    dma = pltpu.SemaphoreType.DMA
    return pl.pallas_call(
        last_kernel,
        out_shape=(
            jax.ShapeDtypeStruct((ROWS, HEADS * WIDE), bf16),
            jax.ShapeDtypeStruct((POOL, BLOCKS, 1024), bf16),
        ),
        in_specs=[IN_VMEM, IN_VMEM],
        out_specs=(IN_VMEM, IN_VMEM),
        scratch_shapes=[
            pltpu.VMEM((4, BLOCKS, 1024), bf16), dma((28,)), dma, dma((4,)), dma((4,)), dma((4,)), dma,
        ],
        compiler_params=pltpu.CompilerParams(
            collective_id=2, has_side_effects=True, vmem_limit_bytes=16 * 1024 * 1024
        ),
        name="last_exchange",
    )(att, dec)


def shards(pool_kv, span_home, span_order, chosen, fresh_q, fresh_kv):
    replica = lax.axis_index("pool")
    my_seat = lax.axis_index("seq")
    home_replica = span_home // 4
    home_slot = span_home % 4
    held = jnp.where(home_replica == replica, home_slot, 0).reshape(POOL, SPANS)
    outgoing = pick_blocks(pool_kv, jnp.sum(held, axis=1).astype(jnp.int32), POOL)
    arrived, qx, fz = first_exchange(outgoing, fresh_q[0], fresh_kv[0])
    lookup = span_order[0][:, None] == jnp.arange(POOL * SPANS, dtype=jnp.int32)[None, :]
    source = jnp.sum(jnp.where(lookup, home_replica[None, :], 0), axis=1).astype(jnp.int32)
    cached = pick_blocks(arrived, source, SPANS)
    kv, fresh = gather_head(cached, fz)
    group = (2 * (my_seat // 8) + my_seat % 2).astype(jnp.int32).reshape(1)
    att, dec = attend(
        chosen[0], group, kv.reshape(32, SPANS, BLOCK, PAIR), fresh.reshape(32 * ROWS, PAIR), qx
    )
    attended, laid = last_exchange(att, dec)
    return attended[None], laid[None, None]


def solution(mesh):
    in_specs = (
        P("pool", "seq", None),
        P(),
        P("pool", None),
        P("pool", None),
        P("pool", "seq", None),
        P("pool", "seq", None),
    )
    out_specs = (P("pool", "seq", None), P("pool", "seq", None, None, None))
    return jax.shard_map(shards, mesh=mesh, in_specs=in_specs, out_specs=out_specs, check_vma=False)
```

```python
import functools
import math

import jax
import jax.numpy as jnp
from jax import lax
from jax.experimental import pallas as pl
from jax.experimental.pallas import tpu as pltpu
from jax.sharding import PartitionSpec as P

MESH = pl.DeviceIdType.MESH
IN_HBM = pl.BlockSpec(memory_space=pltpu.HBM)
IN_VMEM = pl.BlockSpec(memory_space=pltpu.VMEM)

POOL = 4
HEADS = 4
GROUP = 12
DIM = 128
BLOCK = 128
SPANS = 3
ROWS = 56
PICKED = 14
BLOCKS = 96
WIDE = GROUP * DIM
PAIR = 2 * DIM
CHUNK = 8
STEPS = BLOCKS // CHUNK
KEYS = CHUNK * BLOCK
TILE = 16 * GROUP
PAIRS = PICKED // 2
ITEM = 2 * TILE
STRIP = 32
LOW = -1e30


def seat(x, z, c):
    return (x * 4 + z) * 2 + c


def here():
    y = lax.axis_index("pool")
    s = lax.axis_index("seq")
    return y, s, s // 8, (s // 2) % 4, s % 2


def remote(src, dst, send, recv, y, s):
    return pltpu.make_async_remote_copy(
        src_ref=src, dst_ref=dst, send_sem=send, recv_sem=recv, device_id=(y, s), device_id_type=MESH
    )


def greet_plane(barrier, y, s):
    def one(d, carry):
        pl.semaphore_signal(barrier, inc=1, device_id=(y, (s + d) % 32), device_id_type=MESH)
        return carry

    lax.fori_loop(1, 32, one, 0)


SHIFTS = (0, 1, 3, 2)
PIECES = 10
HALF = BLOCK // 2


def exchange_kernel(
    home, order, pool_ref, q_ref, f_ref, qx_ref, all_ref, fr_ref,
    pool_v, out_v, arr_a, arr_b, kv_v, fz_v,
    p_sem, y_send, y_recv, q_send, q_recv, f_send, f_recv, z_send, z_recv,
    x_send, x_recv, h_send, h_recv, c_send, c_recv, l_sem,
):
    y, s, x, z, c = here()
    right, left, far = (x + 1) % 4, (x + 3) % 4, (x + 2) % 4
    across = seat(x, z, 1 - c)
    arrived = (arr_a, arr_b)
    barrier = pltpu.get_barrier_semaphore()
    greet_plane(barrier, y, s)
    for d in range(1, POOL):
        pl.semaphore_signal(barrier, inc=1, device_id=((y + d) % POOL, s), device_id_type=MESH)
    pool_in = pltpu.make_async_copy(pool_ref, pool_v, p_sem.at[0])
    pool_in.start()

    def columns(h):
        return pl.ds(pl.multiple_of(h * PAIR, PAIR), PAIR)

    own_fresh = pltpu.make_async_copy(f_ref.at[:, columns(z)], fz_v.at[z], p_sem.at[1])
    own_fresh.start()
    pool_in.wait()
    for r in range(POOL):
        slot = jnp.int32(0)
        for i in range(3 * r, 3 * r + 3):
            slot = slot + jnp.where(home[i] // 4 == y, home[i] % 4, 0)
        out_v[r] = pool_v[slot]
    for half in range(2):
        arrived[half][y] = out_v[y, half * HALF : (half + 1) * HALF, :]
    pl.semaphore_wait(barrier, 31 + POOL - 1)

    pending = []

    def start(copy):
        copy.start()
        pending.append(copy)
        return copy

    for d in (1, 2, 3):
        to = (z + d) % 4
        start(remote(f_ref.at[:, columns(to)], fz_v.at[z], f_send.at[d - 1], f_recv.at[d - 1], y, seat(x, to, c)))
    fresh = pending[:3]
    passages = [[], []]
    for half in range(2):
        for d in (1, 3, 2):
            to = (y + d) % POOL
            src = out_v.at[to, pl.ds(half * HALF, HALF)]
            copy = remote(src, arrived[half].at[y], y_send.at[half, d - 1], y_recv.at[half, d - 1], to, s)
            passages[half].append(start(copy))

    def piece(t):
        k, h = t // 4, t % 4
        m = 7 * s + k
        g = m % 8
        to = seat(g // 2, h, g % 2)
        src = q_ref.at[pl.ds(pl.multiple_of(k * 8, 8), 8), pl.ds(pl.multiple_of(h * WIDE, WIDE), WIDE)]
        dst = qx_ref.at[pl.ds(pl.multiple_of((m // 8) * 8, 8), 8), :]
        return src, dst, to

    def send(t, carry):
        src, dst, to = piece(t)

        @pl.when(to != s)
        def _():
            remote(src, dst, q_send.at[t], q_recv, y, to).start()

        @pl.when(to == s)
        def _():
            pltpu.make_async_copy(src, dst, q_recv).start()

        return carry

    lax.fori_loop(0, 28, send, 0)

    def view(p, at, core):
        if p < 2:
            return fr_ref.at[at, pl.ds(2 * p, 2), core]
        half, n = (p - 2) // 4, (p - 2) % 4
        return all_ref.at[at, (z + SHIFTS[n]) % 4, core, :, pl.ds(half * HALF, HALF)]

    def origin(p):
        if p < 2:
            return fz_v.at[pl.ds(2 * p, 2)]
        half, n = (p - 2) // 4, (p - 2) % 4
        return kv_v.at[:, pl.ds(half * HALF, HALF), columns(z)] if n == 0 else view(p, x, c)

    def ring(p, way, src):
        to = left if way else right
        return remote(src, view(p, x, c), x_send.at[way, p], x_recv.at[way, p], y, seat(to, z, c))

    def ring_in(p, way):
        v = view(p, right if way else left, c)
        return remote(v, v, x_send.at[way, p], x_recv.at[way, p], y, seat(left, z, c))

    def onward(p):
        at, to = (right, left) if p % 2 else (left, right)
        v = view(p, at, c)
        return remote(v, v, h_send.at[p], h_recv.at[p], y, seat(to, z, c))

    def onward_in(p):
        v = view(p, far, c)
        return remote(v, v, h_send.at[p], h_recv.at[p], y, seat(left, z, c))

    def give(p, kind, core, src=None):
        v = view(p, (x, left, right, far)[kind], core)
        return remote(v if src is None else src, v, c_send.at[kind, p], c_recv.at[kind, p], y, across)

    z_in = {}
    kept = []

    def pick(half):
        for copy in passages[half]:
            copy.wait_recv()
        rows = slice(half * HALF, (half + 1) * HALF)
        for j in range(SPANS):
            kv_v[j, rows, :] = arrived[half][home[order[j]] // 4]
        for d in (1, 3, 2):
            to = (z + d) % 4
            src = kv_v.at[:, pl.ds(half * HALF, HALF), columns(to)]
            dst = all_ref.at[x, z, c, :, pl.ds(half * HALF, HALF)]
            z_in[half, 4 - d] = start(
                remote(src, dst, z_send.at[half, d - 1], z_recv.at[half, d - 1], y, seat(x, to, c))
            )

    def own_ready(p):
        src = origin(p)
        if p >= 2 and (p - 2) % 4:
            z_in[(p - 2) // 4, SHIFTS[(p - 2) % 4]].wait_recv()
        else:
            copy = pltpu.make_async_copy(src, view(p, x, c), l_sem.at[p])
            copy.start()
            kept.append(copy)
        start(ring(p, 0, src))
        start(ring(p, 1, src))
        start(give(p, 0, c, src))

    def passed(p):
        for way in (0, 1):
            ring_in(p, way).wait_recv()
            if p % 2 == way:
                start(onward(p))
            start(give(p, 1 + way, c))

    def beyond(p):
        onward_in(p).wait_recv()
        start(give(p, 3, c))

    own_fresh.wait()
    for copy in fresh:
        copy.wait_recv()
    own_ready(0)
    own_ready(1)
    pick(0)
    own_ready(2)
    passed(0)
    passed(1)
    for p in (3, 4, 5):
        own_ready(p)
    pick(1)
    own_ready(6)
    for p in (2, 3, 4, 5):
        passed(p)
    beyond(0)
    beyond(1)
    for p in (7, 8, 9):
        own_ready(p)
    for p in (6, 7, 8, 9):
        passed(p)
        beyond(p - 4)
    for p in (6, 7, 8, 9):
        beyond(p)

    def sent(t, carry):
        src, dst, to = piece(t)

        @pl.when(to != s)
        def _():
            remote(src, dst, q_send.at[t], q_recv, y, to).wait_send()

        return carry

    lax.fori_loop(0, 28, sent, 0)
    remote(qx_ref, qx_ref, q_send.at[0], q_recv, y, (s + 1) % 32).wait_recv()
    for copy in kept:
        copy.wait()
    for p in range(PIECES):
        for kind in range(4):
            give(p, kind, 1 - c).wait_recv()
    for copy in pending:
        copy.wait_send()


def exchange(home, order, pool_kv, fresh_q, fresh_kv):
    bf16 = jnp.bfloat16
    dma = pltpu.SemaphoreType.DMA
    smem = pl.BlockSpec(memory_space=pltpu.SMEM)
    return pl.pallas_call(
        exchange_kernel,
        out_shape=(
            jax.ShapeDtypeStruct((4 * ROWS, WIDE), bf16),
            jax.ShapeDtypeStruct((4, 4, 2, SPANS, BLOCK, PAIR), bf16),
            jax.ShapeDtypeStruct((4, 4, 2, ROWS, PAIR), bf16),
        ),
        in_specs=[smem, smem, IN_HBM, IN_HBM, IN_HBM],
        out_specs=(IN_VMEM, IN_HBM, IN_HBM),
        scratch_shapes=[
            pltpu.VMEM((4, BLOCK, 1024), bf16),
            pltpu.VMEM((POOL, BLOCK, 1024), bf16),
            pltpu.VMEM((POOL, HALF, 1024), bf16),
            pltpu.VMEM((POOL, HALF, 1024), bf16),
            pltpu.VMEM((SPANS, BLOCK, 1024), bf16),
            pltpu.VMEM((4, ROWS, PAIR), bf16),
            dma((2,)),
            dma((2, 3)),
            dma((2, 3)),
            dma((28,)),
            dma,
            dma((3,)),
            dma((3,)),
            dma((2, 3)),
            dma((2, 3)),
            dma((2, PIECES)),
            dma((2, PIECES)),
            dma((PIECES,)),
            dma((PIECES,)),
            dma((4, PIECES)),
            dma((4, PIECES)),
            dma((PIECES,)),
        ],
        compiler_params=pltpu.CompilerParams(
            collective_id=0, has_side_effects=True, vmem_limit_bytes=16 * 1024 * 1024
        ),
        name="exchange",
    )(home, order, pool_kv, fresh_q, fresh_kv)


def attend_kernel(
    chosen, group, kv_ref, fr_ref, qx_ref, att_ref, dec_ref,
    kv, fresh, q, top, acc, s_a, s_b, w_a, w_b, f_a, f_b, rows32, sems,
):
    g = group[0]
    bf16, f32 = jnp.bfloat16, jnp.float32

    def load(step):
        j, part = step // 4, step % 4
        for side in range(2):
            yield pltpu.make_async_copy(
                kv_ref.at[pl.ds(part * CHUNK, CHUNK), j, :, pl.ds(side * DIM, DIM)],
                kv.at[side, pl.ds(step * CHUNK, CHUNK)],
                sems.at[side, step],
            )

    fresh_in = [
        pltpu.make_async_copy(fr_ref.at[:, pl.ds(side * DIM, DIM)], fresh.at[side], sems.at[side, STEPS])
        for side in range(2)
    ]
    for copy in fresh_in:
        copy.start()
    for step in range(STEPS):
        for copy in load(step):
            copy.start()

    scale = math.log2(math.e) / math.sqrt(DIM)

    def prepare(i, carry):
        r0 = pl.multiple_of(i * 16, 16)
        half = (i % 2) * TILE
        for hd in range(GROUP):
            to = pl.multiple_of(half + hd * 16, 16)
            q[i // 2, pl.ds(to, 16), :] = qx_ref[pl.ds(r0, 16), hd * DIM : (hd + 1) * DIM]
        return carry

    lax.fori_loop(0, PICKED, prepare, 0)

    def clear(p, carry):
        top[p] = jnp.full((ITEM, DIM), LOW, f32)
        acc[p] = jnp.zeros((ITEM, PAIR), f32)
        return carry

    lax.fori_loop(0, PAIRS, clear, 0)
    w_b[...] = jnp.zeros((CHUNK, ITEM, DIM), bf16)
    f_b[...] = jnp.ones((ITEM, DIM), f32)
    for copy in fresh_in:
        copy.wait()

    def before(block):
        total = jnp.int32(0)
        for i in range(PICKED):
            total = total + jnp.where(chosen[i] < block, 1, 0).astype(jnp.int32)
        return total

    def make_ready(step):
        for copy in load(step):
            copy.wait()

        def patch(i, carry):
            for side in range(2):
                kv[side, chosen[i]] = fresh[side, pl.ds(pl.multiple_of(i * BLOCK, BLOCK), BLOCK), :]
            return carry

        lax.fori_loop(before(step * CHUNK), before((step + 1) * CHUNK), patch, 0)
        at = step * CHUNK
        for side in range(2):
            slab = kv[side, pl.ds(at, CHUNK), pl.ds(pl.multiple_of(g * 16, 16), 16), :].astype(f32)
            rows32[side] = slab.reshape(CHUNK * 16, DIM)
        for k in range(4):
            for u in range(4):
                for side in range(2):
                    line = rows32[side, pl.ds(4 * k + u, CHUNK, stride=16), :]
                    to = u * PAIR + side * DIM
                    dec_ref[k, pl.ds(pl.multiple_of(at, CHUNK), CHUNK), to : to + DIM] = line.astype(bf16)

    ones = jnp.ones((KEYS, DIM), bf16)

    def scores(p, step, s):
        keys = kv[0, pl.ds(step * CHUNK, CHUNK)].reshape(KEYS, DIM)
        s[...] = lax.dot_general(q[p], keys, (((1,), (1,)), ((), ())), preferred_element_type=f32)

    def hide(p, step, s, dead):
        for side in range(2):
            rows = slice(side * TILE, (side + 1) * TILE)
            own = jnp.where(dead, -1, chosen[2 * p + side] - step * CHUNK)

            def blank(j, carry):
                s[rows, pl.ds(pl.multiple_of(j * BLOCK, BLOCK), BLOCK)] = jnp.full((TILE, BLOCK), LOW, f32)
                return carry

            lax.fori_loop(jnp.clip(own + 1, 0, CHUNK), CHUNK, blank, 0)

            @pl.when(jnp.logical_and(own >= 0, own < CHUNK))
            def _():
                cols = pl.ds(pl.multiple_of(own * BLOCK, BLOCK), BLOCK)
                row = lax.broadcasted_iota(jnp.int32, (TILE, BLOCK), 0)
                token = 64 * ((row % 16) // 8) + 8 * g + row % 8
                key = lax.broadcasted_iota(jnp.int32, (TILE, BLOCK), 1)
                s[rows, cols] = jnp.where(key <= token, s[rows, cols], LOW)

    def soften(p, s, w, f, lo, hi):
        for r in range(lo, hi, STRIP):
            rows = slice(r, r + STRIP)
            parts = [s[rows, j * DIM : (j + 1) * DIM] for j in range(CHUNK)]
            best = functools.reduce(jnp.maximum, parts)
            old = top[p, rows, :]
            new = jnp.maximum(old, jnp.max(best, axis=1, keepdims=True))
            for j in range(CHUNK):
                w[j, rows, :] = jnp.exp2((parts[j] - new) * scale).astype(bf16)
            f[rows, :] = jnp.exp2((old - new) * scale)
            top[p, rows, :] = new

    def mix(p, step, w, f, lo, hi):
        values = jnp.concatenate([kv[1, pl.ds(step * CHUNK, CHUNK)].reshape(KEYS, DIM), ones], axis=1)
        weights = jnp.concatenate([w[j, lo:hi, :] for j in range(CHUNK)], axis=1)
        part = jnp.dot(weights, values, preferred_element_type=f32)
        factor = f[lo:hi, :]
        acc[p, lo:hi, :] = acc[p, lo:hi, :] * jnp.concatenate([factor, factor], axis=1) + part

    def last_of(p):
        return chosen[2 * p + 1] // CHUNK

    total = jnp.int32(0)
    for p in range(PAIRS):
        total = total + last_of(p) + 1

    def following(item):
        p, step = item
        more = step < last_of(p)
        return (
            jnp.where(more, p, jnp.minimum(p + 1, PAIRS - 1)),
            jnp.where(more, step + 1, 0),
        )

    def turn(t, ready, last, now, s_now, s_next, w_now, w_last, f_now, f_last):
        after = following(now)
        fits = after[1] < ready

        @pl.when(jnp.logical_not(fits))
        def _():
            make_ready(after[1])

        dead = t >= total
        @pl.when(jnp.logical_or(dead, chosen[2 * now[0]] < (now[1] + 1) * CHUNK))
        def _():
            hide(now[0], now[1], s_now, dead)

        scores(after[0], after[1], s_next)
        for lo in range(0, ITEM, TILE):
            soften(now[0], s_now, w_now, f_now, lo, lo + TILE)
            mix(now[0], now[1], w_now, f_now, lo, lo + TILE)
        return jnp.where(fits, ready, after[1] + 1), now, after

    def both_turns(i, carry):
        ready, last, now = carry
        ready, last, now = turn(2 * i, ready, last, now, s_a, s_b, w_a, w_b, f_a, f_b)
        ready, last, now = turn(2 * i + 1, ready, last, now, s_b, s_a, w_b, w_a, f_b, f_a)
        return ready, last, now

    make_ready(0)
    zero = jnp.int32(0)
    scores(0, 0, s_a)
    ready, last, now = lax.fori_loop(0, (total + 1) // 2, both_turns, (jnp.int32(1), (zero, zero), (zero, zero)))

    def rest(step, carry):
        make_ready(step)
        return carry

    lax.fori_loop(ready, STEPS, rest, 0)

    def finish(i, carry):
        half = (i % 2) * TILE
        r0 = pl.multiple_of(i * 16, 16)
        for hd in range(GROUP):
            rows = pl.ds(pl.multiple_of(half + hd * 16, 16), 16)
            out = acc[i // 2, rows, 0:DIM] / acc[i // 2, rows, DIM:PAIR]
            att_ref[pl.ds(r0, 16), hd * DIM : (hd + 1) * DIM] = out.astype(bf16)
        return carry

    lax.fori_loop(0, PICKED, finish, 0)


def attend(chosen, group, kv, fresh, qx):
    bf16, f32 = jnp.bfloat16, jnp.float32
    smem = pl.BlockSpec(memory_space=pltpu.SMEM)
    return pl.pallas_call(
        attend_kernel,
        out_shape=(
            jax.ShapeDtypeStruct((4 * ROWS, WIDE), bf16),
            jax.ShapeDtypeStruct((4, BLOCKS, 1024), bf16),
        ),
        in_specs=[smem, smem, IN_HBM, IN_HBM, IN_VMEM],
        out_specs=(IN_VMEM, IN_VMEM),
        scratch_shapes=[
            pltpu.VMEM((2, BLOCKS, BLOCK, DIM), bf16),
            pltpu.VMEM((2, PICKED * BLOCK, DIM), bf16),
            pltpu.VMEM((PAIRS, ITEM, DIM), bf16),
            pltpu.VMEM((PAIRS, ITEM, DIM), f32),
            pltpu.VMEM((PAIRS, ITEM, PAIR), f32),
            pltpu.VMEM((ITEM, KEYS), f32),
            pltpu.VMEM((ITEM, KEYS), f32),
            pltpu.VMEM((CHUNK, ITEM, DIM), bf16),
            pltpu.VMEM((CHUNK, ITEM, DIM), bf16),
            pltpu.VMEM((ITEM, DIM), f32),
            pltpu.VMEM((ITEM, DIM), f32),
            pltpu.VMEM((2, CHUNK * 16, DIM), f32),
            pltpu.SemaphoreType.DMA((2, STEPS + 1)),
        ],
        compiler_params=pltpu.CompilerParams(vmem_limit_bytes=40 * 1024 * 1024),
        name="attend",
    )(chosen, group, kv, fresh, qx)


def last_kernel(
    att_ref, dec_ref, out_ref, laid_ref, mid, a_send, a_recv, z_send, z_recv, y_send, y_recv
):
    y, s, x, z, c = here()
    g = 2 * x + c
    barrier = pltpu.get_barrier_semaphore()
    greet_plane(barrier, y, s)
    for d in range(1, POOL):
        pl.semaphore_signal(barrier, inc=1, device_id=((y + d) % POOL, s), device_id_type=MESH)
    pl.semaphore_wait(barrier, 31 + POOL - 1)

    def slab(k):
        to_z, to_c = 2 * c + k // 2, k % 2
        return dec_ref.at[k], mid.at[z], seat(x, to_z, to_c)

    def slab_send(k, carry):
        src, dst, to = slab(k)

        @pl.when(to != s)
        def _():
            remote(src, dst, z_send.at[k], z_recv.at[z], y, to).start()

        @pl.when(to == s)
        def _():
            pltpu.make_async_copy(src, dst, z_recv.at[z]).start()

        return carry

    lax.fori_loop(0, 4, slab_send, 0)

    def piece(j):
        m = 8 * j + g
        src = att_ref.at[pl.ds(pl.multiple_of(j * 8, 8), 8), :]
        dst = out_ref.at[
            pl.ds(pl.multiple_of((m % 7) * 8, 8), 8), pl.ds(pl.multiple_of(z * WIDE, WIDE), WIDE)
        ]
        return src, dst, m // 7

    def send(j, carry):
        src, dst, to = piece(j)

        @pl.when(to != s)
        def _():
            remote(src, dst, a_send.at[j], a_recv, y, to).start()

        @pl.when(to == s)
        def _():
            pltpu.make_async_copy(src, dst, a_recv).start()

        return carry

    lax.fori_loop(0, 28, send, 0)

    passing = []
    for d in (0, 1, 3, 2):
        h = (z + d) % 4
        remote(mid.at[h], mid.at[h], y_send.at[d], z_recv.at[h], y, (s + 1) % 32).wait_recv()
        copy = remote(mid.at[h], laid_ref.at[y], y_send.at[d], y_recv, h, s)
        own = pltpu.make_async_copy(mid.at[h], laid_ref.at[y], y_recv)

        @pl.when(h != y)
        def _():
            copy.start()

        @pl.when(h == y)
        def _():
            own.start()

        passing.append((h, copy))

    def slab_sent(k, carry):
        src, dst, to = slab(k)

        @pl.when(to != s)
        def _():
            remote(src, dst, z_send.at[k], z_recv.at[z], y, to).wait_send()

        return carry

    lax.fori_loop(0, 4, slab_sent, 0)

    def sent(j, carry):
        src, dst, to = piece(j)

        @pl.when(to != s)
        def _():
            remote(src, dst, a_send.at[j], a_recv, y, to).wait_send()

        return carry

    lax.fori_loop(0, 28, sent, 0)
    for h, copy in passing:

        @pl.when(h != y)
        def _():
            copy.wait_send()

    remote(out_ref, out_ref, a_send.at[0], a_recv, y, (s + 1) % 32).wait_recv()
    remote(laid_ref, laid_ref, y_send.at[0], y_recv, y, (s + 1) % 32).wait_recv()


def last_exchange(att, dec):
    bf16 = jnp.bfloat16
    dma = pltpu.SemaphoreType.DMA
    return pl.pallas_call(
        last_kernel,
        out_shape=(
            jax.ShapeDtypeStruct((ROWS, HEADS * WIDE), bf16),
            jax.ShapeDtypeStruct((POOL, BLOCKS, 1024), bf16),
        ),
        in_specs=[IN_VMEM, IN_VMEM],
        out_specs=(IN_VMEM, IN_VMEM),
        scratch_shapes=[
            pltpu.VMEM((4, BLOCKS, 1024), bf16), dma((28,)), dma, dma((4,)), dma((4,)), dma((4,)), dma,
        ],
        compiler_params=pltpu.CompilerParams(
            collective_id=2, has_side_effects=True, vmem_limit_bytes=16 * 1024 * 1024
        ),
        name="last_exchange",
    )(att, dec)


def shards(pool_kv, span_home, span_order, chosen, fresh_q, fresh_kv):
    my_seat = lax.axis_index("seq")
    qx, kv, fresh = exchange(span_home, span_order[0], pool_kv, fresh_q[0], fresh_kv[0])
    group = (2 * (my_seat // 8) + my_seat % 2).astype(jnp.int32).reshape(1)
    att, dec = attend(
        chosen[0], group, kv.reshape(32, SPANS, BLOCK, PAIR), fresh.reshape(32 * ROWS, PAIR), qx
    )
    attended, laid = last_exchange(att, dec)
    return attended[None], laid[None, None]


def solution(mesh):
    in_specs = (
        P("pool", "seq", None),
        P(),
        P("pool", None),
        P("pool", None),
        P("pool", "seq", None),
        P("pool", "seq", None),
    )
    out_specs = (P("pool", "seq", None), P("pool", "seq", None, None, None))
    return jax.shard_map(shards, mesh=mesh, in_specs=in_specs, out_specs=out_specs, check_vma=False)
```
